32 devices in a mesh: visit: 4 (over y, x), ccd: 8 (over z, core).
Axes of the slice: x: 2, y: 2, z: 4, core: 2. Of those that a mesh axis runs over, the one named last changes fastest.
Arguments:
- exposure: bfloat16 [4, 512, 4096], P('visit', 'ccd'), may hold values from -6 to 6
- offsets: int32 [4, 8, 2], P('visit', 'ccd'), may hold values from -32 to 32
- fraction: float32 [4, 8, 2], P('visit', 'ccd'), may hold values from 0 to 1
- route_patch: int32 [4, 512], P('visit', 'ccd'), may hold values from 0 to 31, as said below
- route_slot: int32 [4, 512], P('visit', 'ccd'), may hold values from 0 to 63
- block_weight: bfloat16 [4, 512], P('visit', 'ccd'), may hold values from 0.25 to 4
- kernel_rows: float32 [33], replicated, may hold values from -1 to 1
- kernel_columns: float32 [33], replicated, may hold values from -1 to 1
Outputs:
- coadded: bfloat16 [512, 16384], P('visit', 'ccd')
- matched: float32 [512, 16384], P('visit', 'ccd')
The draws below stay inside these ranges and needn't reach their ends.
Inputs may be any that keep to these rules, and one draw needn't show every extreme that they name: `route_patch`: no patch is named by more than 8 of one exposure's 64 blocks; one patch, drawn from the seed, is named by exactly 8 blocks of every exposure.
All inputs are finite; a program needn't handle non-finite values.
Results may differ from the reference program's by a relative error of at most 0.0082.
Values may be sent and summed in bfloat16 or wider, within the bound.
No kernel may reach another device: no remote copies, remote signals or barrier semaphores. Data moves between devices by JAX's collectives and lax.ppermute only.
A program may use at most 64 MiB of HBM per device.

```python
import math
import jax
import jax.numpy as jnp
from jax import lax

COLS = 4096
ROWS_DEV = 64
BLOCK_ROWS = 32
BLOCK_COLS = 128
MAX_OFFSET = 32
MARGIN = 40
HALF_KERNEL = 16
VISITS = 4
CCDS = 8
PATCHES = 32
FOCAL_ROWS = 512
BLOCKS = 64
CAP = 8
SLOTS = 64
PATCH_ROWS = 128
PATCH_COLS = 2048
SLOT_ROWS = 4
SLOT_COLS = 16
TAPS = 33


def draw_route_patch(key, part):
    deep_key, rest_key = jax.random.split(jax.random.fold_in(key, 11))
    deepest = jax.random.randint(deep_key, (), 0, PATCHES)

    def one_source(source_key):
        count_key, order_key, place_key = jax.random.split(source_key, 3)
        others = jax.random.permutation(order_key, PATCHES - 1).astype(jnp.int32)
        others = others + (others >= deepest).astype(jnp.int32)
        counts = jax.random.randint(count_key, (PATCHES - 1,), CAP // 2, CAP + 1)
        ends = jnp.cumsum(counts)
        position = jnp.arange(BLOCKS - CAP, dtype=jnp.int32)
        which = jnp.sum((position[:, None] >= ends[None, :]).astype(jnp.int32), axis=1)
        listed = jnp.concatenate([jnp.full((CAP,), deepest, jnp.int32), others[which].astype(jnp.int32)])
        shuffle = jax.random.permutation(place_key, BLOCKS)
        return listed[shuffle]
    source_keys = jax.random.split(rest_key, PATCHES)
    routes = jax.vmap(one_source)(source_keys)
    return routes.reshape(VISITS, CCDS * BLOCKS).astype(jnp.int32)


def set_ends(result, rng, least, largest):
    longest = result.shape.index(max(result.shape))
    spots = []
    for shift in (0, 1):
        where = [jax.random.randint(jax.random.fold_in(rng, axis), (), 0, length) for axis, length in enumerate(result.shape)]
        where[longest] = (where[longest] + shift) % result.shape[longest]
        spots.append(tuple(where))
    return result.at[spots[0]].set(least).at[spots[1]].set(largest)


def block_levels(rng, shape, pieces, smallest, high):
    level = 1.0
    for dim, parts in pieces:
        steps = jax.random.uniform(jax.random.fold_in(jax.random.fold_in(rng, 6), dim), (parts,), jnp.float32, smallest / len(pieces), high / len(pieces))
        level = level * jnp.repeat(jnp.exp(steps), shape[dim] // parts).reshape((-1,) + (1,) * (len(shape) - 1 - dim))
    return level


def bell_draw(rng, shape, deviation, limit, cuts=(), held_as=jnp.bfloat16):
    gain = block_levels(rng, shape, cuts, -0.22, 0.18) if cuts else 1.0
    values = jax.random.normal(rng, shape, jnp.float32) * deviation * gain
    return jnp.minimum(jnp.maximum(values, -limit), limit).astype(held_as)


def setup_inputs(seed: int = 0) -> dict:
    keys = jax.random.split(jax.random.key(seed), 9)
    exposure = bell_draw(keys[0], (VISITS, FOCAL_ROWS, COLS), 1.0, 6.0, ((0, 4), (1, 8)))
    offsets = set_ends(jax.random.randint(keys[1], (VISITS, CCDS, 2), 0 - MAX_OFFSET, MAX_OFFSET + 1), jax.random.fold_in(keys[1], 1), 0 - MAX_OFFSET, MAX_OFFSET).astype(jnp.int32)
    fraction = jnp.clip(1.0 * jax.random.uniform(keys[2], (VISITS, CCDS, 2), jnp.float32) ** block_levels(keys[2], (VISITS, CCDS, 2), ((0, 4), (1, 8)), -0.2, 0.2), 0.0, 1.0)
    route_patch = draw_route_patch(jax.random.fold_in(keys[8], 71), 0)
    route_slot = set_ends(jax.random.randint(keys[4], (VISITS, CCDS * BLOCKS), 0, SLOTS), jax.random.fold_in(keys[4], 1), 0, SLOTS - 1).astype(jnp.int32)
    block_weight = jnp.clip(jnp.exp(math.log(4.0) - 2.7725887 * jax.random.uniform(keys[5], (VISITS, CCDS * BLOCKS), jnp.float32) ** block_levels(keys[5], (VISITS, CCDS * BLOCKS), ((0, 4), (1, 8)), -0.2, 0.2)), 0.25, 4.0).astype(jnp.bfloat16)
    kernel_rows = bell_draw(keys[6], (TAPS,), TAPS ** -0.5, 1.0, (), jnp.float32)
    kernel_columns = bell_draw(keys[7], (TAPS,), TAPS ** -0.5, 1.0, (), jnp.float32)
    return {"exposure": exposure, "offsets": offsets, "fraction": fraction, "route_patch": route_patch, "route_slot": route_slot, "block_weight": block_weight, "kernel_rows": kernel_rows, "kernel_columns": kernel_columns}


def lanczos_weights(fraction_part):
    distance = jnp.arange(3, -3, -1).astype(jnp.float32) - fraction_part
    kernel = jnp.sinc(distance) * jnp.sinc(distance / 3.0)
    return (kernel / jnp.sum(kernel)).astype(jnp.bfloat16)


def reference(exposure, offsets, fraction, route_patch, route_slot, block_weight, kernel_rows, kernel_columns):
    padded = jnp.pad(exposure, ((0, 0), (MARGIN, MARGIN), (0, 0)))

    def warp_one(source):
        visit_index = source // CCDS
        ccd_index = source % CCDS
        shift_rows = offsets[visit_index, ccd_index, 0].astype(jnp.int32)
        shift_columns = offsets[visit_index, ccd_index, 1].astype(jnp.int32)
        row_weights = lax.optimization_barrier(lanczos_weights(fraction[visit_index, ccd_index, 0])).astype(jnp.float32)
        column_weights = lax.optimization_barrier(lanczos_weights(fraction[visit_index, ccd_index, 1])).astype(jnp.float32)
        focal = lax.dynamic_index_in_dim(padded, visit_index, 0, keepdims=False)
        summed = jnp.zeros((ROWS_DEV, COLS), jnp.float32)
        for tap_index in range(6):
            first_row = (ccd_index * ROWS_DEV + MARGIN - shift_rows - (3 - tap_index)).astype(jnp.int32)
            summed = summed + row_weights[tap_index] * lax.dynamic_slice_in_dim(focal, first_row, ROWS_DEV, 0).astype(jnp.float32)
        row_warped = summed.astype(jnp.bfloat16)
        widened = jnp.pad(row_warped, ((0, 0), (128, 128)))
        summed = jnp.zeros((ROWS_DEV, COLS), jnp.float32)
        for tap_index in range(6):
            first_column = (128 - shift_columns - (3 - tap_index)).astype(jnp.int32)
            summed = summed + column_weights[tap_index] * lax.dynamic_slice_in_dim(widened, first_column, COLS, 1).astype(jnp.float32)
        return summed.astype(jnp.bfloat16)

    warped = lax.map(warp_one, jnp.arange(PATCHES, dtype=jnp.int32))
    blocks = warped.reshape(PATCHES, ROWS_DEV // BLOCK_ROWS, BLOCK_ROWS, COLS // BLOCK_COLS, BLOCK_COLS)
    blocks = blocks.transpose(0, 1, 3, 2, 4).reshape(PATCHES * BLOCKS, BLOCK_ROWS * BLOCK_COLS)
    destination = (route_patch.reshape(-1) * SLOTS + route_slot.reshape(-1)).astype(jnp.int32)
    weights = block_weight.reshape(-1).astype(jnp.float32)
    numerator = jax.ops.segment_sum(blocks.astype(jnp.float32) * weights[:, None], destination, num_segments=PATCHES * SLOTS)
    weight_total = jax.ops.segment_sum(weights, destination, num_segments=PATCHES * SLOTS)
    slot_values = (numerator / jnp.maximum(weight_total, 1.0)[:, None]).astype(jnp.bfloat16)
    coadded = slot_values.reshape(VISITS, CCDS, SLOT_ROWS, SLOT_COLS, BLOCK_ROWS, BLOCK_COLS)
    coadded = coadded.transpose(0, 2, 4, 1, 3, 5).reshape(VISITS * PATCH_ROWS, CCDS * PATCH_COLS)
    row_kernel = lax.optimization_barrier(kernel_rows.astype(jnp.bfloat16)).astype(jnp.float32)
    column_kernel = lax.optimization_barrier(kernel_columns.astype(jnp.bfloat16)).astype(jnp.float32)
    framed = jnp.pad(coadded, HALF_KERNEL)
    tract_rows = VISITS * PATCH_ROWS
    tract_columns = CCDS * PATCH_COLS
    summed = jnp.zeros((tract_rows, tract_columns + 2 * HALF_KERNEL), jnp.float32)
    for tap_index in range(TAPS):
        summed = summed + row_kernel[tap_index] * framed[tap_index:tap_index + tract_rows].astype(jnp.float32)
    smoothed = summed.astype(jnp.bfloat16)
    matched = jnp.zeros((tract_rows, tract_columns), jnp.float32)
    for tap_index in range(TAPS):
        matched = matched + column_kernel[tap_index] * smoothed[:, tap_index:tap_index + tract_columns].astype(jnp.float32)
    return coadded, matched
```

```python
import functools

import jax
import jax.numpy as jnp
from jax import lax
from jax.experimental import pallas as pl
from jax.experimental.pallas import tpu as pltpu
from jax.sharding import Mesh, PartitionSpec as P

BLOCK_ROWS = 32
BLOCK_COLS = 128
MARGIN = 40
HALF_KERNEL = 16
LANES = 128
WIDE = 256
GROUP = 16
F32 = jnp.float32
BF16 = jnp.bfloat16
VMEM = pl.BlockSpec(memory_space=pltpu.VMEM)
SMEM = pl.BlockSpec(memory_space=pltpu.SMEM)


def dot(a, b):
    return jnp.dot(a, b, preferred_element_type=F32)


def iota(shape, axis):
    return lax.broadcasted_iota(jnp.int32, shape, axis)


def shaped(*shape, dtype=BF16):
    return jax.ShapeDtypeStruct(shape, dtype)


def cost(flops, moved):
    return pl.CostEstimate(flops=flops, bytes_accessed=moved, transcendentals=0)


def sinc(x):
    angle = jnp.pi * x
    safe = jnp.where(angle == 0.0, 1.0, angle)
    return jnp.where(angle == 0.0, 1.0, jnp.sin(safe) / safe)


def lanczos_taps(part):
    tap = iota((1, LANES), 1)
    distance = 3.0 - tap.astype(F32) - part
    kernel = jnp.where(tap < 6, sinc(distance) * sinc(distance / 3.0), 0.0)
    kernel = (kernel / jnp.sum(kernel, axis=1, keepdims=True)).astype(BF16).astype(F32)
    return [jnp.sum(jnp.where(tap == k, kernel, 0.0), axis=1, keepdims=True) for k in range(6)]


def band(lag, taps):
    matrix = jnp.zeros(lag.shape, F32)
    for k, tap in enumerate(taps):
        matrix = jnp.where(lag == k, tap, matrix)
    return matrix.astype(BF16)


def warp_matrices_kernel(offset_ref, part_ref, before_ref, own_ref, after_ref, column_ref):
    rows = own_ref.shape[0]
    row_taps = lanczos_taps(part_ref[0])
    first = MARGIN - 3 - offset_ref[0]
    for ref, start in ((before_ref, 0), (own_ref, MARGIN), (after_ref, MARGIN + rows)):
        lag = iota(ref.shape, 1) - iota(ref.shape, 0) + (start - first)
        ref[...] = band(lag, row_taps)
    column_taps = lanczos_taps(part_ref[1])
    lag = iota(column_ref.shape, 0) - iota(column_ref.shape, 1) - (LANES - 3 - offset_ref[1])
    column_ref[...] = band(lag, column_taps)


def warp_matrices(offset, part, rows):
    return pl.pallas_call(
        warp_matrices_kernel,
        out_shape=(
            shaped(rows, MARGIN),
            shaped(rows, rows),
            shaped(rows, MARGIN),
            shaped(WIDE + 2 * LANES, WIDE),
        ),
        in_specs=[SMEM, SMEM],
        out_specs=(VMEM,) * 4,
        cost_estimate=cost(2_000_000, 400_000),
        name="warp_matrices",
    )(offset, part)


def warp_kernel(
    pixel_ref, before_ref, after_ref, row_b_ref, row_o_ref, row_a_ref, column_ref, out_ref,
    padded, ordered,
):
    rows, columns = pixel_ref.shape
    blocks = (rows // BLOCK_ROWS) * (columns // BLOCK_COLS)
    across = columns // BLOCK_COLS
    padded[:, :LANES] = jnp.zeros((rows, LANES), BF16)
    padded[:, LANES + columns :] = jnp.zeros((rows, LANES), BF16)
    step = 2 * WIDE
    for start in range(0, columns, step):
        where = slice(start, start + step)
        summed = dot(row_o_ref[...], pixel_ref[:, where])
        summed += dot(row_b_ref[...], before_ref[:, where])
        summed += dot(row_a_ref[...], after_ref[:, where])
        padded[:, LANES + start : LANES + start + step] = summed.astype(BF16)
    for start in range(0, columns, WIDE):
        warped = dot(padded[:, start : start + WIDE + 2 * LANES], column_ref[...])
        for piece in range(WIDE // BLOCK_COLS):
            j = start // BLOCK_COLS + piece
            for i in range(rows // BLOCK_ROWS):
                ordered[pl.ds(i * across + j, BLOCK_ROWS, stride=blocks), :] = warped[
                    i * BLOCK_ROWS : (i + 1) * BLOCK_ROWS,
                    piece * BLOCK_COLS : (piece + 1) * BLOCK_COLS,
                ]
    out_ref[...] = ordered[...].astype(BF16)


def warp(pixels, before, after, matrices):
    rows, columns = pixels.shape
    total = rows * columns // BLOCK_COLS
    return pl.pallas_call(
        warp_kernel,
        out_shape=shaped(total, BLOCK_COLS),
        in_specs=[VMEM] * 7,
        out_specs=VMEM,
        scratch_shapes=[
            pltpu.VMEM((rows, columns + 2 * LANES), BF16),
            pltpu.VMEM((total, BLOCK_COLS), F32),
        ],
        cost_estimate=cost(700_000_000, 4_000_000),
        name="warp",
    )(pixels, before, after, *matrices)


def route_kernel(
    here_ref, table_ref, place_ref, tag_ref, *, owners_across, dests, capacity, tag_rows, tag_each
):
    blocks = table_ref.shape[1]
    half_across = owners_across // 2
    patch_l = jnp.broadcast_to(table_ref[0:1, :], (blocks, blocks))
    slot_l = jnp.broadcast_to(table_ref[1:2, :], (blocks, blocks))
    weight_l = jnp.broadcast_to(table_ref[2:3, :], (blocks, blocks))
    down, along = iota((blocks, blocks), 0), iota((blocks, blocks), 1)

    def upright(rows):
        return jnp.sum(jnp.where(down == along, rows, 0.0), axis=1, keepdims=True)

    patch_s = upright(patch_l)
    same = (patch_s == patch_l).astype(F32)
    rank_l = jnp.sum(jnp.where(down < along, same, 0.0), axis=0, keepdims=True)
    rank_s = jnp.sum(jnp.where(along < down, same, 0.0), axis=1, keepdims=True)
    patch = table_ref[0:1, :].astype(jnp.int32)
    visit = lax.div(patch, jnp.int32(owners_across))
    column = patch - visit * owners_across - here_ref[0] * half_across
    inside = (column >= 0) & (column < half_across)
    dest = jnp.where(inside, visit * half_across + column, -1)
    rank = rank_l.astype(jnp.int32)

    together = GROUP // capacity
    rows = iota(place_ref.shape[:1] + (blocks,), 0)
    row_dest = lax.div(rows, jnp.int32(GROUP))
    row_in = rows - row_dest * GROUP
    row_part = lax.div(row_in, jnp.int32(capacity))
    hit = (row_dest == dest) & (row_in - row_part * capacity == rank)
    place_ref[...] = jnp.concatenate(
        [(hit & (row_part == part)).astype(F32) for part in range(together)], axis=1
    ).astype(BF16)

    kinds = 2 * tag_each
    rows = iota((dests * tag_rows, blocks), 0)
    row_dest = lax.div(rows, jnp.int32(tag_rows))
    row_kind = rows - row_dest * tag_rows
    left = jnp.concatenate(
        [((row_dest == dest) & (row_kind == kind)).astype(F32) for kind in range(kinds)], axis=1
    ).astype(BF16)
    lane = iota((blocks, LANES), 1)
    pieces = []
    for kind in range(kinds):
        number = lane + (kind % tag_each) * LANES
        source = lax.div(number, jnp.int32(GROUP))
        turn = lax.rem(number, jnp.int32(capacity))
        match = (source == here_ref[1]) & (turn == rank_s.astype(jnp.int32))
        value = upright(slot_l if kind < tag_each else weight_l)
        pieces.append(jnp.where(match, value, 0.0))
    right = jnp.concatenate(pieces, axis=0).astype(BF16)
    tag_ref[...] = dot(left, right).astype(BF16)


def route(here, table, sizes):
    owners_across, dests, capacity, tag_rows, tag_each = sizes
    blocks = table.shape[1]
    body = functools.partial(
        route_kernel,
        owners_across=owners_across,
        dests=dests,
        capacity=capacity,
        tag_rows=tag_rows,
        tag_each=tag_each,
    )
    return pl.pallas_call(
        body,
        out_shape=(
            shaped(dests * GROUP, GROUP // capacity * blocks),
            shaped(dests * tag_rows, LANES),
        ),
        in_specs=[SMEM, VMEM],
        out_specs=(VMEM, VMEM),
        cost_estimate=cost(4_000_000, 200_000),
        name="route",
    )(here, table)


def place_kernel(block_ref, place_ref, tag_ref, out_ref):
    dests, rows, _ = out_ref.shape
    depth = place_ref.shape[1]
    groups = block_ref.shape[0] // depth
    placing = place_ref[...]
    for group in range(0, groups, 2):
        pair = jnp.concatenate(
            [block_ref[(group + n) * depth : (group + n + 1) * depth, :] for n in range(2)], axis=1
        )
        placed = dot(placing, pair).astype(BF16)
        for n in range(2):
            out_ref[:, (group + n) * GROUP : (group + n + 1) * GROUP, :] = placed[
                :, n * LANES : (n + 1) * LANES
            ].reshape(dests, GROUP, LANES)
    tags = rows - groups * GROUP
    out_ref[:, groups * GROUP :, :] = tag_ref[...].reshape(dests, tags, LANES)


def place(blocks, placing, tags):
    dests = placing.shape[0] // GROUP
    rows = blocks.shape[0] // placing.shape[1] * GROUP + tags.shape[0] // dests
    return pl.pallas_call(
        place_kernel,
        out_shape=shaped(dests, rows, LANES),
        in_specs=[VMEM] * 3,
        out_specs=VMEM,
        cost_estimate=cost(300_000_000, 2_000_000),
        name="place",
    )(blocks, placing, tags)


def coadd_kernel(*refs, tag_rows, tag_each, capacity, slots):
    *got_refs, out_ref, top_ref, bottom_ref, ordered = refs
    sources, rows, _ = got_refs[0].shape
    together = GROUP // capacity
    groups = (rows - tag_rows) // GROUP
    across = out_ref.shape[1] // BLOCK_COLS
    weights, total = [], 0.0
    depth = sources * GROUP
    for got in got_refs:
        tags = jnp.sum(got[:, rows - tag_rows :, :].astype(F32), axis=0)
        slot = jnp.concatenate([tags[n : n + 1] for n in range(tag_each)], axis=1)
        weight = jnp.concatenate([tags[tag_each + n : tag_each + n + 1] for n in range(tag_each)], axis=1)
        shape = (together * slots, depth)
        row, lane = iota(shape, 0), iota(shape, 1)
        part = lax.div(row, jnp.int32(slots))
        lane_part = lax.div(lax.rem(lane, jnp.int32(GROUP)), jnp.int32(capacity))
        match = ((row - part * slots) == slot.astype(jnp.int32)) & (part == lane_part)
        matrix = jnp.where(match, weight, 0.0)
        total = total + jnp.sum(matrix, axis=1, keepdims=True)
        weights.append(matrix.astype(BF16))
    divisor = jnp.maximum(total, 1.0)
    for group in range(0, groups, 2):
        summed = 0.0
        for got, matrix in zip(got_refs, weights):
            pair = jnp.concatenate(
                [
                    got[:, (group + n) * GROUP : (group + n + 1) * GROUP, :].reshape(depth, LANES)
                    for n in range(2)
                ],
                axis=1,
            )
            summed = summed + dot(matrix, pair)
        value = summed / divisor
        for n in range(2):
            for part in range(together):
                r = (group + n) * together + part
                ordered[pl.ds(r, slots, stride=BLOCK_ROWS), :] = value[
                    part * slots : (part + 1) * slots, n * LANES : (n + 1) * LANES
                ]
    for q in range(slots):
        y, x = q // across * BLOCK_ROWS, q % across * BLOCK_COLS
        out_ref[y : y + BLOCK_ROWS, x : x + BLOCK_COLS] = ordered[
            q * BLOCK_ROWS : (q + 1) * BLOCK_ROWS, :
        ].astype(BF16)
    patch_rows = out_ref.shape[0]
    top_ref[...] = out_ref[:HALF_KERNEL, :]
    bottom_ref[...] = out_ref[patch_rows - HALF_KERNEL :, :]


def coadd(gots, patch, sizes, slots):
    _, _, capacity, tag_rows, tag_each = sizes
    body = functools.partial(
        coadd_kernel, tag_rows=tag_rows, tag_each=tag_each, capacity=capacity, slots=slots
    )
    return pl.pallas_call(
        body,
        out_shape=(shaped(*patch), shaped(HALF_KERNEL, patch[1]), shaped(HALF_KERNEL, patch[1])),
        in_specs=[VMEM] * len(gots),
        out_specs=(VMEM,) * 3,
        scratch_shapes=[pltpu.VMEM((slots * BLOCK_ROWS, BLOCK_COLS), F32)],
        cost_estimate=cost(600_000_000, 4_000_000),
        name="coadd",
    )(*gots)


def filters_kernel(row_taps_ref, column_taps_ref, top_ref, own_ref, bottom_ref, column_ref):
    rows = own_ref.shape[0]
    taps = [row_taps_ref[k] for k in range(row_taps_ref.shape[0])]
    for ref, start in ((top_ref, 0), (own_ref, HALF_KERNEL), (bottom_ref, HALF_KERNEL + rows)):
        ref[...] = band(iota(ref.shape, 1) - iota(ref.shape, 0) + start, taps)
    taps = [column_taps_ref[k] for k in range(column_taps_ref.shape[0])]
    lag = iota(column_ref.shape, 0) - iota(column_ref.shape, 1) - (LANES - HALF_KERNEL)
    column_ref[...] = band(lag, taps)


def filters(row_taps, column_taps, patch_rows):
    return pl.pallas_call(
        filters_kernel,
        out_shape=(
            shaped(patch_rows, HALF_KERNEL),
            shaped(patch_rows, patch_rows),
            shaped(patch_rows, HALF_KERNEL),
            shaped(WIDE + 2 * LANES, WIDE),
        ),
        in_specs=[SMEM, SMEM],
        out_specs=(VMEM,) * 4,
        cost_estimate=cost(10_000_000, 400_000),
        name="filters",
    )(row_taps, column_taps)


def match_kernel(
    own_ref, above_ref, below_ref, row_t_ref, row_o_ref, row_b_ref, column_ref, out_ref, padded
):
    rows, columns = own_ref.shape
    padded[:, :LANES] = jnp.zeros((rows, LANES), BF16)
    padded[:, LANES + columns :] = jnp.zeros((rows, LANES), BF16)
    step = 2 * WIDE
    for start in range(0, columns, step):
        where = slice(start, start + step)
        summed = dot(row_o_ref[...], own_ref[:, where])
        summed += dot(row_t_ref[...], above_ref[:, where])
        summed += dot(row_b_ref[...], below_ref[:, where])
        padded[:, LANES + start : LANES + start + step] = summed.astype(BF16)
    for start in range(0, columns, WIDE):
        out_ref[:, start : start + WIDE] = dot(
            padded[:, start : start + WIDE + 2 * LANES], column_ref[...]
        )


def match(coadded, above, below, filter_set):
    rows, columns = coadded.shape
    return pl.pallas_call(
        match_kernel,
        out_shape=shaped(rows, columns, dtype=F32),
        in_specs=[VMEM] * 7,
        out_specs=VMEM,
        scratch_shapes=[pltpu.VMEM((rows, columns + 2 * LANES), BF16)],
        cost_estimate=cost(700_000_000, 4_000_000),
        name="match",
    )(coadded, above, below, *filter_set)


def edge_kernel(frame_ref, row_t_ref, row_o_ref, row_b_ref, column_ref, matched_ref, out_ref):
    frame = frame_ref[0]
    rows = row_o_ref.shape[0]
    smoothed = dot(row_o_ref[...], frame[HALF_KERNEL : HALF_KERNEL + rows])
    smoothed += dot(row_t_ref[...], frame[:HALF_KERNEL])
    smoothed += dot(row_b_ref[...], frame[HALF_KERNEL + rows :])
    out_ref[...] = matched_ref[...] + dot(smoothed.astype(BF16), column_ref[...])


def add_edges(matched, frames, filter_set):
    rows, columns = matched.shape
    last = columns // LANES - 1
    row_t, row_o, row_b, column = filter_set
    depth = column.shape[0] // LANES - 1

    def whole(array):
        return pl.BlockSpec(array.shape, lambda side: (0, 0))

    edge = pl.BlockSpec((rows, LANES), lambda side: (0, side * last))
    return pl.pallas_call(
        edge_kernel,
        grid=(2,),
        out_shape=shaped(rows, columns, dtype=F32),
        in_specs=[
            pl.BlockSpec((1,) + frames.shape[1:], lambda side: (side, 0, 0)),
            whole(row_t),
            whole(row_o),
            whole(row_b),
            pl.BlockSpec((LANES, LANES), lambda side: (side * depth, side)),
            edge,
        ],
        out_specs=edge,
        input_output_aliases={5: 0},
        cost_estimate=cost(30_000_000, 300_000),
        name="edges",
    )(frames, row_t, row_o, row_b, column, matched)


def neighbours(x_up, x_down, axis):
    devices = 1
    for name in axis:
        devices *= lax.axis_size(name)
    up = [(i, i + 1) for i in range(devices - 1)]
    down = [(j, i) for i, j in up]
    return lax.ppermute(x_up, axis, up), lax.ppermute(x_down, axis, down)


def on_device(
    exposure, offsets, fraction, route_patch, route_slot, block_weight, kernel_rows, kernel_columns
):
    pixels = exposure[0]
    rows, columns = pixels.shape
    across = ("half", "rest")
    before, after = neighbours(pixels[rows - MARGIN :], pixels[:MARGIN], across)

    blocks = route_patch.shape[1]
    visits, halves, rest = (lax.axis_size(name) for name in ("visit", "half", "rest"))
    owners_across = halves * rest
    dests = visits * rest
    capacity = 4 * blocks // (visits * owners_across)
    tag_each = dests * GROUP // LANES
    tag_rows = max(8, 2 * tag_each)
    sizes = (owners_across, dests, capacity, tag_rows, tag_each)
    table = jnp.concatenate(
        [route_patch.astype(F32), route_slot.astype(F32), block_weight.astype(F32)], axis=0
    )
    swap = [(i, halves - 1 - i) for i in range(halves)]
    other_table = lax.ppermute(table, "half", swap)
    here = jnp.stack(
        [lax.axis_index("half"), lax.axis_index("visit") * rest + lax.axis_index("rest")]
    ).astype(jnp.int32)
    matrices = warp_matrices(offsets.reshape(-1), fraction.reshape(-1), rows)
    placing, tags = route(here, table, sizes)

    warped = warp(pixels, before, after, matrices)
    other_warped = lax.ppermute(warped, "half", swap)
    group = ("visit", "rest")
    own_got = lax.all_to_all(place(warped, placing, tags), group, 0, 0, tiled=True)
    other_placing, other_tags = route(here, other_table, sizes)
    filter_set = filters(kernel_rows, kernel_columns, 2 * rows)
    other_got = lax.all_to_all(
        place(other_warped, other_placing, other_tags), group, 0, 0, tiled=True
    )
    patch = (2 * rows, columns // 2)
    coadded, top, bottom = coadd((own_got, other_got), patch, sizes, blocks)

    above, below = neighbours(bottom, top, ("visit",))
    ends = [
        jnp.concatenate([above[:, s], coadded[:, s], below[:, s]], axis=0)
        for s in (slice(patch[1] - LANES, patch[1]), slice(0, LANES))
    ]
    matched = match(coadded, above, below, filter_set)
    frames = jnp.stack(neighbours(ends[0], ends[1], across))
    matched = add_edges(matched, frames, filter_set)
    return (coadded, matched)


def solution(mesh):
    visits, ccds = (mesh.shape[name] for name in ("visit", "ccd"))
    split = Mesh(mesh.devices.reshape(visits, 2, ccds // 2), ("visit", "half", "rest"))
    ccd = ("half", "rest")
    placed = (
        P("visit", ccd, None),
        P("visit", ccd, None),
        P("visit", ccd, None),
        P("visit", ccd),
        P("visit", ccd),
        P("visit", ccd),
        P(),
        P(),
    )
    return jax.shard_map(
        on_device,
        mesh=split,
        in_specs=placed,
        out_specs=(P("visit", ccd), P("visit", ccd)),
        check_vma=False,
    )
```
